256 devices in a mesh: sector: 128 (over z, y_lo, x, core), blk: 2 (over y_hi).
Axes of the slice: x: 4, y: 4 (y_hi: 2, y_lo: 2; y = y_hi * 2 + y_lo), z: 8, core: 2. Of those that a mesh axis runs over, the one named last changes fastest.
Arguments:
- signal: bfloat16 [4, 4096, 8192], P('blk', 'sector'), may hold values from -6 to 6
- offsets: int32 [4], P('blk'), may hold values from 0 to 4095
- fraction: float32 [4, 8192], P('blk'), may hold values from 0 to 1
- radius: float32 [256], replicated, may hold values from 0.2 to 0.9
- azimuth: float32 [256], replicated, may hold values from -3.140625 to 3.140625
Outputs:
- power: float32 [512, 256], P(('sector', 'blk'))
The draws below stay inside these ranges and needn't reach their ends.
All inputs are finite; a program needn't handle non-finite values.
Results may differ from the reference program's by a relative error of at most 0.00095.
Values may be sent and summed in bfloat16 or wider, within the bound.
No kernel may reach another device: no remote copies, remote signals or barrier semaphores. Data moves between devices by JAX's collectives and lax.ppermute only.
A program may use at most 64 MiB of HBM per device.

```python
import math
import jax
import jax.numpy as jnp
from jax import lax

MICS = 4096
NFFT = 1024
NBIN = 512
SAMPLES = 8192
BLOCKS = 4
SEGS = 15
GRID = 256


def touch_ends(values, own_key, smallest, largest):
    longest = values.shape.index(max(values.shape))
    spots = []
    for shift in (0, 1):
        where = [jax.random.randint(jax.random.fold_in(own_key, axis), (), 0, length) for axis, length in enumerate(values.shape)]
        where[longest] = (where[longest] + shift) % values.shape[longest]
        spots.append(tuple(where))
    return values.at[spots[0]].set(smallest).at[spots[1]].set(largest)


def block_scale(stream_key, shape, cuts, least, high):
    def one(dim, parts):
        steps = jax.random.uniform(jax.random.fold_in(jax.random.fold_in(stream_key, 6), dim), (parts,), jnp.float32, least / len(cuts), high / len(cuts))
        return jnp.repeat(jnp.exp(steps), shape[dim] // parts).reshape((-1,) + (1,) * (len(shape) - dim - 1))

    level = one(*cuts[0])
    for cut in cuts[1:]:
        level = level * one(*cut)
    return level


def gaussian(stream_key, shape, deviation, bound, pieces=(), kind=jnp.bfloat16):
    drawn = jax.random.normal(stream_key, shape, jnp.float32) * deviation
    if len(pieces) > 0:
        drawn = block_scale(stream_key, shape, pieces, -0.22, 0.18) * drawn
    return jnp.clip(drawn, min=-bound, max=bound).astype(kind)


def setup_inputs(seed: int = 0) -> dict:
    streams_of = jax.random.split(jax.random.key(seed), 6)
    signal = gaussian(streams_of[0], (BLOCKS, MICS, SAMPLES), 1.0, 6.0, ((0, 2), (1, 128)))
    offsets = touch_ends(jax.random.randint(streams_of[1], (BLOCKS,), 0, MICS), jax.random.fold_in(streams_of[1], 1), 0, MICS - 1).astype(jnp.int32)
    fraction = jnp.clip(1.0 * jax.random.uniform(streams_of[2], (BLOCKS, SAMPLES), jnp.float32) ** block_scale(streams_of[2], (BLOCKS, SAMPLES), ((0, 2),), -0.2, 0.2), 0.0, 1.0)
    radius = jnp.clip(jax.random.uniform(streams_of[3], (GRID,), jnp.float32, 0.2, 0.9), 0.2, 0.9)
    azimuth = jnp.clip(jax.random.uniform(streams_of[4], (GRID,), jnp.float32, -3.140625, 3.140625), -3.140625, 3.140625)
    return {"signal": signal, "offsets": offsets, "fraction": fraction, "radius": radius, "azimuth": azimuth}


wavenumber = 2.0
height = 0.5

def fourier_table(groups):
    half_bins = NFFT // 2
    per_group = half_bins // groups
    sample = lax.iota(jnp.int32, NFFT)[:, None]
    column = lax.iota(jnp.int32, 2 * half_bins)[None, :]
    group = column // (2 * per_group)
    part = column // per_group % 2
    inner = column % per_group
    frequency = group * per_group + inner
    turns = (sample * frequency % NFFT).astype(jnp.float32)
    angle = turns * (2.0 * math.pi / NFFT)
    window = 0.5 - 0.5 * jnp.cos(sample.astype(jnp.float32) * (2.0 * math.pi / NFFT))
    value = jnp.where(part == 0, jnp.cos(angle), -jnp.sin(angle))
    return (value * window / math.sqrt(3.0 * NFFT / 8.0)).astype(jnp.bfloat16)

def distances(radius, azimuth, total_mics):
    turn = lax.iota(jnp.int32, total_mics).astype(jnp.float32) * (2.0 * math.pi / total_mics)
    cycle_cos = jnp.cos(turn)[:, None]
    cycle_sin = jnp.sin(turn)[:, None]
    across = (radius * jnp.cos(azimuth))[None, :]
    along = (radius * jnp.sin(azimuth))[None, :]
    squared = 1.0 + height * height + (radius * radius)[None, :] - 2.0 * (cycle_cos * across + cycle_sin * along)
    return jnp.sqrt(squared)

def steering(frequency, distance):
    phase = wavenumber * frequency.astype(jnp.float32) * distance
    return jnp.concatenate([jnp.cos(phase), jnp.sin(phase)], 1).astype(jnp.bfloat16)

def reference(signal, offsets, fraction, radius, azimuth):
    table = fourier_table(1).astype(jnp.float32)
    half = NFFT // 2

    def one_block(inputs):
        rows_in, start, weight = inputs
        doubled = jnp.concatenate([rows_in, rows_in], 0)
        window_rows = lax.dynamic_slice_in_dim(doubled, start.astype(jnp.int32), MICS + 1, 0).astype(jnp.float32)
        mixed = (1.0 - weight[None, :]) * window_rows[:-1] + weight[None, :] * window_rows[1:]
        virtual = lax.optimization_barrier(mixed.astype(jnp.bfloat16)).astype(jnp.float32)
        halves = virtual.reshape(MICS, SAMPLES // half, half)
        upper = jnp.einsum('mhn,nc->hcm', halves[:, :-1], table[:half], precision=lax.Precision.HIGHEST)
        lower = jnp.einsum('mhn,nc->hcm', halves[:, 1:], table[half:], precision=lax.Precision.HIGHEST)
        return (upper + lower).astype(jnp.bfloat16)
    spectra = lax.map(one_block, (signal, offsets, fraction))
    distance = distances(radius, azimuth, MICS)
    snapshot_count = BLOCKS * SEGS
    flat = spectra.reshape(snapshot_count, 2 * NBIN, MICS)

    def one_bin(frequency):
        real_part = lax.dynamic_index_in_dim(flat, frequency, 1, keepdims=False).astype(jnp.float32)
        imag_part = lax.dynamic_index_in_dim(flat, frequency + NBIN, 1, keepdims=False).astype(jnp.float32)
        steer = steering(frequency, distance).astype(jnp.float32)
        from_real = jnp.dot(real_part, steer, precision=lax.Precision.HIGHEST)
        from_imag = jnp.dot(imag_part, steer, precision=lax.Precision.HIGHEST)
        along = from_real[:, :GRID] + from_imag[:, GRID:]
        across = from_imag[:, :GRID] - from_real[:, GRID:]
        return lax.optimization_barrier(jnp.sum(along * along + across * across, 0)) / (MICS * snapshot_count)
    return lax.map(one_bin, jnp.arange(NBIN, dtype=jnp.int32))
```

```python
import math

import jax
import jax.numpy as jnp
import numpy as np
from jax import lax
from jax.experimental import pallas as pl
from jax.experimental.pallas import tpu as pltpu
from jax.sharding import PartitionSpec as P

NFFT = 1024
HALF = NFFT // 2
LANES = 128
GROUP = 8

wavenumber = 2.0
height = 0.5

f32 = jnp.float32
bf16 = jnp.bfloat16


def fourier_tables(owners):
    sample = np.arange(NFFT)[None, :]
    per_owner = HALF // owners
    inner = np.arange(per_owner)[:, None, None]
    part = np.arange(2)[None, :, None]
    owner = np.arange(owners)[None, None, :]
    frequency = (owner * per_owner + inner + 0 * part).reshape(-1, 1)
    kind = (0 * owner + 0 * inner + part).reshape(-1, 1)
    angle = (sample * frequency % NFFT) * (2.0 * math.pi / NFFT)
    window = 0.5 - 0.5 * np.cos(sample * (2.0 * math.pi / NFFT))
    value = np.where(kind == 0, np.cos(angle), -np.sin(angle)) * window / math.sqrt(3.0 * NFFT / 8.0)
    value = value.astype(np.float32).astype(bf16)
    return value[:, :HALF], value[:, HALF:]


def spectra_body(offsets_ref, signal_ref, fraction_ref, upper_ref, lower_ref, out_ref, up_ref, low_ref, wide_ref):
    blocks, mics, length = signal_ref.shape
    halves = length // HALF
    owners = out_ref.shape[0]
    slot = blocks * halves
    rows = GROUP * slot
    lane = lax.broadcasted_iota(jnp.int32, (1, LANES), 1)
    row8 = lax.broadcasted_iota(jnp.int32, (GROUP, 1), 0)
    for group in range(mics // GROUP):
        base = group * GROUP
        for b in range(blocks):
            for h in range(halves):
                place = pl.ds(b * halves + h, GROUP, stride=slot)
                for q in range(HALF // LANES):
                    cols = slice(h * HALF + q * LANES, h * HALF + (q + 1) * LANES)
                    weight = fraction_ref[b : b + 1, cols]
                    here = signal_ref[b, base : base + GROUP, cols].astype(f32)
                    shifted = pltpu.roll(here, GROUP - 1, 0)
                    if base + GROUP < mics:
                        after = signal_ref[b, base + GROUP : base + GROUP + 1, cols].astype(f32)
                    else:
                        after = jnp.zeros((1, LANES), f32)
                    following = jnp.where(row8 == GROUP - 1, after, shifted)
                    mixed = (1.0 - weight) * here + weight * following
                    if h < halves - 1:
                        up_ref[q, place, :] = mixed
                    if h > 0:
                        low_ref[q, place, :] = mixed
        for m in range(GROUP):
            segment = base + m
            for b in range(blocks):
                top = m * slot + b * halves + halves - 1
                bottom = (top + 1) % rows
                if segment < halves - 1:
                    for ref, place, h in ((up_ref, top, segment), (low_ref, bottom, segment + 1)):
                        for q in range(HALF // LANES):
                            cols = slice(h * HALF + q * LANES, h * HALF + (q + 1) * LANES)
                            first = signal_ref[b, 0:1, cols].astype(f32)
                            ref[q, place : place + 1, :] = fraction_ref[b : b + 1, cols] * first
                else:
                    for q in range(HALF // LANES):
                        up_ref[q, top : top + 1, :] = jnp.zeros((1, LANES), f32)
                        low_ref[q, bottom : bottom + 1, :] = jnp.zeros((1, LANES), f32)
        contract = (((1,), (1,)), ((), ()))
        samples_up = jnp.concatenate([up_ref[q].astype(bf16) for q in range(HALF // LANES)], 1)
        samples_low = jnp.concatenate([low_ref[q].astype(bf16) for q in range(HALF // LANES)], 1)
        upper = lax.dot_general(upper_ref[...], samples_up, contract, preferred_element_type=f32)
        lower = lax.dot_general(lower_ref[...], samples_low, contract, preferred_element_type=f32)
        total = upper + pltpu.roll(lower, rows - 1, 1)
        for tile in range(rows // LANES):
            part = [total[c * owners : (c + 1) * owners, tile * LANES : (tile + 1) * LANES] for c in range(4)]
            for bit in (0, 1):
                step = slot << bit
                odd = (lane // step) % 2 == 1
                for c in range(4):
                    if c >> bit & 1 == 0:
                        a, z = part[c], part[c | 1 << bit]
                        part[c] = jnp.where(odd, pltpu.roll(z, step, 1), a)
                        part[c | 1 << bit] = jnp.where(odd, z, pltpu.roll(a, LANES - step, 1))
            for r in range(4):
                m = base + tile * 4 + r
                value = part[r]
                if m in (halves, halves + 1):
                    numbers = []
                    for b in range(blocks):
                        offset = offsets_ref[b]
                        numbers.append((offset // mics if m == halves else offset % mics).astype(f32))
                    note = jnp.where(lane // halves % 2 == 0, numbers[0], numbers[1])
                    value = jnp.where(lane % halves == halves - 1, note, value)
                wide_ref[pl.ds(m, owners, stride=mics), :] = value
    for owner in range(0, owners, 32):
        piece = wide_ref[owner * mics : (owner + 32) * mics, :]
        out_ref[owner : owner + 32] = piece.astype(bf16).reshape(32, mics, LANES)


def local_spectra(signal, offsets, fraction, owners):
    blocks, mics, length = signal.shape
    rows = GROUP * blocks * (length // HALF)
    upper, lower = fourier_tables(owners)
    vmem = pl.BlockSpec(memory_space=pltpu.VMEM)
    return pl.pallas_call(
        spectra_body,
        out_shape=jax.ShapeDtypeStruct((owners, mics, LANES), bf16),
        in_specs=[pl.BlockSpec(memory_space=pltpu.SMEM), vmem, vmem, vmem, vmem],
        out_specs=vmem,
        scratch_shapes=[
            pltpu.VMEM((HALF // LANES, rows, LANES), f32),
            pltpu.VMEM((HALF // LANES, rows, LANES), f32),
            pltpu.VMEM((owners * mics, LANES), f32),
        ],
        name="spectra",
    )(offsets, signal, fraction, jnp.asarray(upper), jnp.asarray(lower))


def cos_sin(phase):
    turns = jnp.round(phase * (1.0 / math.pi))
    rest = phase - turns * 3.140625
    rest = rest - turns * 9.67502593994140625e-4
    rest = rest - turns * 1.509957990978376432e-7
    half = turns * 0.5
    sign = 1.0 - 4.0 * (half - jnp.floor(half))
    square = rest * rest
    cosine = 1.0 / math.factorial(12)
    for order in (10, 8, 6, 4, 2, 0):
        cosine = cosine * square + (-1.0) ** (order // 2) / math.factorial(order)
    sine = -1.0 / math.factorial(11)
    for order in (9, 7, 5, 3, 1):
        sine = sine * square + (-1.0) ** (order // 2) / math.factorial(order)
    return sign * cosine, sign * rest * sine


STEER_COLS = 512


def steer_body(first_ref, cycle_ref, base_ref, across_ref, along_ref, out_ref):
    points = base_ref.shape[0]
    bins = out_ref.shape[0] // (2 * points)
    first = first_ref[0]
    cycle_cos = cycle_ref[0:1, :]
    cycle_sin = cycle_ref[1:2, :]

    def rows16(i, _):
        rows = pl.ds(pl.multiple_of(i * 16, 16), 16)
        squared = base_ref[rows, :] - 2.0 * (cycle_cos * across_ref[rows, :] + cycle_sin * along_ref[rows, :])
        distance = jnp.sqrt(squared)
        for j in range(bins):
            phase = wavenumber * (first + j).astype(f32) * distance
            cosine, sine = cos_sin(phase)
            place = pl.multiple_of(2 * j * points + i * 16, 16)
            out_ref[pl.ds(place, 16), :] = cosine.astype(bf16)
            place = pl.multiple_of((2 * j + 1) * points + i * 16, 16)
            out_ref[pl.ds(place, 16), :] = sine.astype(bf16)
        return 0

    lax.fori_loop(0, points // 16, rows16, 0)


def steering(first, bins, radius, azimuth, total_mics):
    turn = lax.iota(jnp.int32, total_mics).astype(f32) * (2.0 * math.pi / total_mics)
    cycle = jnp.stack([jnp.cos(turn), jnp.sin(turn)])
    points = radius.shape[0]
    base = (1.0 + height * height + radius * radius)[:, None]
    across = (radius * jnp.cos(azimuth))[:, None]
    along = (radius * jnp.sin(azimuth))[:, None]
    column = pl.BlockSpec((points, 1), lambda i: (0, 0))
    return pl.pallas_call(
        steer_body,
        grid=(total_mics // STEER_COLS,),
        out_shape=jax.ShapeDtypeStruct((bins * 2 * points, total_mics), bf16),
        in_specs=[
            pl.BlockSpec(memory_space=pltpu.SMEM),
            pl.BlockSpec((2, STEER_COLS), lambda i: (0, i)),
            column,
            column,
            column,
        ],
        out_specs=pl.BlockSpec((bins * 2 * points, STEER_COLS), lambda i: (0, i)),
        name="steer",
    )(first.reshape(1), cycle, base, across, along)


BEAM_ROWS = 512


def beam_body(received_ref, steer_ref, out_ref, wide_ref, start_ref, sum_ref, *, mics, blocks, halves, scale):
    step = pl.program_id(0)
    sources, groups = received_ref.shape[0], received_ref.shape[1]
    total = sources * mics
    lane = lax.broadcasted_iota(jnp.int32, (1, LANES), 1)
    spare = lane % halves == halves - 1
    of_block = lane // halves % blocks

    @pl.when(step == 0)
    def _():
        for group in range(groups):
            for source in range(0, sources, 16):
                piece = received_ref[source : source + 16, group].astype(f32).reshape(16 * mics, LANES)
                wide_ref[group, source * mics : (source + 16) * mics, :] = piece
            head = wide_ref[group, 0:mics, :]
            which = lax.broadcasted_iota(jnp.int32, (mics, LANES), 0)
            for b in range(blocks):
                mine = spare & (of_block == b) & (lane // (blocks * halves) == 0)
                hop = jnp.sum(jnp.where(mine & (which == halves), head, 0.0))
                within = jnp.sum(jnp.where(mine & (which == halves + 1), head, 0.0))
                start_ref[group * blocks + b] = hop.astype(jnp.int32) * mics + within.astype(jnp.int32)
            carried = jnp.zeros((sources, LANES), f32)
            for segment in range(halves - 1):
                rows = wide_ref[group, pl.ds(segment, sources, stride=mics), :]
                moved = pltpu.roll(jnp.where(spare, rows, 0.0), LANES - (halves - 1 - segment), 1)
                carried = carried + moved
            carried = pltpu.roll(carried, sources - 1, 0)
            last = pl.ds(mics - 1, sources, stride=mics)
            whole = wide_ref[group, last, :] + carried
            wide_ref[group, last, :] = whole
            wide_ref[group, total : total + BEAM_ROWS, :] = wide_ref[group, 0:BEAM_ROWS, :]
        sum_ref[...] = jnp.zeros(sum_ref.shape, f32)

    pieces = []
    for group in range(groups):
        start = [(start_ref[group * blocks + b] + step * BEAM_ROWS) % total for b in range(blocks)]
        rows = [wide_ref[group, pl.ds(s, BEAM_ROWS), :] for s in start]
        pieces.append(jnp.where(of_block == 0, rows[0], rows[1]).astype(bf16))
    stacked = jnp.concatenate(pieces, 1)
    sum_ref[...] += jnp.dot(steer_ref[...], stacked, preferred_element_type=f32)

    @pl.when(step == pl.num_programs(0) - 1)
    def _():
        points = out_ref.shape[1]
        slot = blocks * halves
        imaginary = lane // slot % 2 == 1
        for j in range(out_ref.shape[0]):
            power = jnp.zeros((points, LANES), f32)
            for group in range(groups):
                cols = slice(group * LANES, (group + 1) * LANES)
                by_cos = sum_ref[2 * j * points : (2 * j + 1) * points, cols]
                by_sin = sum_ref[(2 * j + 1) * points : (2 * j + 2) * points, cols]
                other = jnp.where(imaginary, -pltpu.roll(by_sin, slot, 1), pltpu.roll(by_sin, LANES - slot, 1))
                both = by_cos + other
                power = power + both * both
            power = jnp.where(~spare & (lane // (2 * slot) == j), power, 0.0)
            out_ref[j : j + 1, :] = jnp.sum(power.T, 0, keepdims=True) * scale


def beam(received, steer, mics, blocks, halves, points, scale):
    sources, groups = received.shape[:2]
    total = sources * mics
    bins = steer.shape[0] // (2 * points)
    body = lambda *refs: beam_body(*refs, mics=mics, blocks=blocks, halves=halves, scale=scale)
    return pl.pallas_call(
        body,
        grid=(total // BEAM_ROWS,),
        out_shape=jax.ShapeDtypeStruct((bins, points), f32),
        in_specs=[
            pl.BlockSpec(received.shape, lambda i: (0, 0, 0, 0)),
            pl.BlockSpec((steer.shape[0], BEAM_ROWS), lambda i: (0, i)),
        ],
        out_specs=pl.BlockSpec((bins, points), lambda i: (0, 0)),
        scratch_shapes=[
            pltpu.VMEM((groups, total + BEAM_ROWS, LANES), f32),
            pltpu.SMEM((groups * blocks,), jnp.int32),
            pltpu.VMEM((steer.shape[0], groups * LANES), f32),
        ],
        name="beam",
    )(received, steer)


def local(signal, offsets, fraction, radius, azimuth):
    blocks, mics, length = signal.shape
    sectors, groups = lax.axis_size("sector"), lax.axis_size("blk")
    owners = sectors * groups
    halves = length // HALF
    bins = HALF // owners
    spectra = local_spectra(signal, offsets, fraction, owners)
    moved = lax.all_to_all(spectra, ("sector", "blk"), split_axis=0, concat_axis=0, tiled=True)
    received = moved.reshape(sectors, groups, mics, LANES)
    first = (lax.axis_index("sector") * groups + lax.axis_index("blk")) * bins
    total_mics = sectors * mics
    steer = steering(first, bins, radius, azimuth, total_mics)
    scale = 1.0 / (total_mics * blocks * (halves - 1) * groups)
    return beam(received, steer, mics, blocks, halves, radius.shape[0], scale)


def solution(mesh):
    return jax.shard_map(
        local,
        mesh=mesh,
        in_specs=(P("blk", "sector", None), P("blk"), P("blk", None), P(), P()),
        out_specs=P(("sector", "blk"), None),
        check_vma=False,
    )
```

```python
import math

import jax
import jax.numpy as jnp
import numpy as np
from jax import lax
from jax.experimental import pallas as pl
from jax.experimental.pallas import tpu as pltpu
from jax.sharding import PartitionSpec as P

NFFT = 1024
HALF = NFFT // 2
LANES = 128

wavenumber = 2.0
height = 0.5

f32 = jnp.float32
bf16 = jnp.bfloat16


def fourier_table(owners):
    sample = np.arange(NFFT)[:, None]
    per_owner = HALF // owners
    in_group = LANES // (2 * per_owner)
    column = np.arange(2 * HALF)[None, :]
    owner = column // LANES * in_group + column % in_group
    part = column // in_group % 2
    frequency = owner * per_owner + column % LANES // (2 * in_group)
    angle = (sample * frequency % NFFT) * (2.0 * math.pi / NFFT)
    window = 0.5 - 0.5 * np.cos(sample * (2.0 * math.pi / NFFT))
    value = np.where(part == 0, np.cos(angle), -np.sin(angle)) * window / math.sqrt(3.0 * NFFT / 8.0)
    return value.astype(np.float32).astype(bf16)


ROWS = 16
TABLE_COLS = 256


def gather_rows(signal_ref, fraction_ref, rows_ref):
    blocks, mics, length = signal_ref.shape
    halves = length // HALF
    row = lax.broadcasted_iota(jnp.int32, (mics, 1), 0)

    def place(part, b, segment):
        first = ((part * blocks + b) * halves + segment) * ROWS
        return slice(first, first + ROWS)

    for b in range(blocks):
        for h in range(halves):
            cols = slice(h * HALF, (h + 1) * HALF)
            weight = fraction_ref[b : b + 1, cols]
            here = signal_ref[b, :, cols].astype(f32)
            following = jnp.where(row == mics - 1, 0.0, pltpu.roll(here, mics - 1, 0))
            mixed = ((1.0 - weight) * here + weight * following).astype(bf16)
            for part in range(mics // ROWS):
                piece = mixed[part * ROWS : (part + 1) * ROWS]
                if h < halves - 1:
                    rows_ref[place(part, b, h), :HALF] = piece
                if h > 0:
                    rows_ref[place(part, b, h - 1), HALF:] = piece
        share = jnp.zeros((ROWS, NFFT), f32)
        for segment in range(halves - 1):
            cols = slice(segment * HALF, segment * HALF + NFFT)
            first = fraction_ref[b : b + 1, cols] * signal_ref[b, 0:1, cols].astype(f32)
            share = jnp.where(row[:ROWS] == segment, first, share)
        rows_ref[place(0, b, halves - 1), :] = share.astype(bf16)
        for part in range(1, mics // ROWS):
            rows_ref[place(part, b, halves - 1), :] = jnp.zeros((ROWS, NFFT), bf16)


def spectra_body(offsets_ref, signal_ref, fraction_ref, table_ref, out_ref, rows_ref):
    blocks, mics, length = signal_ref.shape
    halves = length // HALF
    slot = blocks * halves
    lane = lax.broadcasted_iota(jnp.int32, (ROWS, LANES), 1)
    row = lax.broadcasted_iota(jnp.int32, (ROWS, LANES), 0)

    @pl.when(pl.program_id(0) == 0)
    def _():
        gather_rows(signal_ref, fraction_ref, rows_ref)

    for part in range(mics // ROWS):
        rows = rows_ref[part * slot * ROWS : (part + 1) * slot * ROWS, :]
        product = jnp.dot(rows, table_ref[...], preferred_element_type=f32)
        for tile in range(TABLE_COLS // LANES):
            pieces = [product[i * ROWS : (i + 1) * ROWS, tile * LANES : (tile + 1) * LANES] for i in range(slot)]
            if part == 1:
                for b in range(blocks):
                    i = b * halves + halves - 1
                    hop = (offsets_ref[b] // mics).astype(f32)
                    within = (offsets_ref[b] % mics).astype(f32)
                    pieces[i] = jnp.where(row == 0, hop, jnp.where(row == 1, within, pieces[i]))
            pieces = [piece.astype(bf16) for piece in pieces]
            step = 1
            while step < slot:
                odd = lane // step % 2 == 1
                for i in range(slot):
                    if i & step == 0:
                        a, z = pieces[i], pieces[i | step]
                        pieces[i] = jnp.where(odd, pltpu.roll(z, step, 1), a)
                        pieces[i | step] = jnp.where(odd, z, pltpu.roll(a, LANES - step, 1))
                step *= 2
            for i in range(slot):
                out_ref[tile * slot + i, part * ROWS : (part + 1) * ROWS, :] = pieces[i].astype(bf16)


def local_spectra(signal, offsets, fraction, owners):
    blocks, mics, length = signal.shape
    rows = mics * blocks * (length // HALF)
    per_step = owners * TABLE_COLS // NFFT
    return pl.pallas_call(
        spectra_body,
        grid=(NFFT // TABLE_COLS,),
        out_shape=jax.ShapeDtypeStruct((owners, mics, LANES), bf16),
        in_specs=[
            pl.BlockSpec(memory_space=pltpu.SMEM),
            pl.BlockSpec(signal.shape, lambda i: (0, 0, 0)),
            pl.BlockSpec(fraction.shape, lambda i: (0, 0)),
            pl.BlockSpec((NFFT, TABLE_COLS), lambda i: (0, i)),
        ],
        out_specs=pl.BlockSpec((per_step, mics, LANES), lambda i: (i, 0, 0)),
        scratch_shapes=[pltpu.VMEM((rows, NFFT), bf16)],
        name="spectra",
    )(offsets, signal, fraction, jnp.asarray(fourier_table(owners)))


def cos_sin(phase):
    turns = jnp.round(phase * (1.0 / math.pi))
    rest = phase - turns * 3.140625
    rest = rest - turns * 9.67502593994140625e-4
    rest = rest - turns * 1.509957990978376432e-7
    half = turns * 0.5
    sign = 1.0 - 4.0 * (half - jnp.floor(half))
    square = rest * rest
    cosine = 1.0 / math.factorial(12)
    for order in (10, 8, 6, 4, 2, 0):
        cosine = cosine * square + (-1.0) ** (order // 2) / math.factorial(order)
    sine = -1.0 / math.factorial(11)
    for order in (9, 7, 5, 3, 1):
        sine = sine * square + (-1.0) ** (order // 2) / math.factorial(order)
    return sign * cosine, sign * rest * sine


STEER_COLS = 512


def steer_body(first_ref, cycle_ref, base_ref, across_ref, along_ref, out_ref):
    points = base_ref.shape[0]
    bins = out_ref.shape[0] // (2 * points)
    first = first_ref[0]
    cycle_cos = cycle_ref[0:1, :]
    cycle_sin = cycle_ref[1:2, :]

    def rows16(i, _):
        rows = pl.ds(pl.multiple_of(i * 16, 16), 16)
        squared = base_ref[rows, :] - 2.0 * (cycle_cos * across_ref[rows, :] + cycle_sin * along_ref[rows, :])
        distance = jnp.sqrt(squared)
        for j in range(bins):
            phase = wavenumber * (first + j).astype(f32) * distance
            cosine, sine = cos_sin(phase)
            place = pl.multiple_of(2 * j * points + i * 16, 16)
            out_ref[pl.ds(place, 16), :] = cosine.astype(bf16)
            place = pl.multiple_of((2 * j + 1) * points + i * 16, 16)
            out_ref[pl.ds(place, 16), :] = sine.astype(bf16)
        return 0

    lax.fori_loop(0, points // 16, rows16, 0)


def steering(first, bins, radius, azimuth, total_mics):
    turn = lax.iota(jnp.int32, total_mics).astype(f32) * (2.0 * math.pi / total_mics)
    cycle = jnp.stack([jnp.cos(turn), jnp.sin(turn)])
    points = radius.shape[0]
    base = (1.0 + height * height + radius * radius)[:, None]
    across = (radius * jnp.cos(azimuth))[:, None]
    along = (radius * jnp.sin(azimuth))[:, None]
    column = pl.BlockSpec((points, 1), lambda i: (0, 0))
    return pl.pallas_call(
        steer_body,
        grid=(total_mics // STEER_COLS,),
        out_shape=jax.ShapeDtypeStruct((bins * 2 * points, total_mics), bf16),
        in_specs=[
            pl.BlockSpec(memory_space=pltpu.SMEM),
            pl.BlockSpec((2, STEER_COLS), lambda i: (0, i)),
            column,
            column,
            column,
        ],
        out_specs=pl.BlockSpec((bins * 2 * points, STEER_COLS), lambda i: (0, i)),
        name="steer",
    )(first.reshape(1), cycle, base, across, along)


BEAM_ROWS = 1024
PIECE = 512
LANDINGS = 4


def beam_body(moved_ref, steer_ref, out_ref, land_ref, wide_ref, start_ref, sum_ref, copied, *, mics, blocks, halves, groups, scale):
    step = pl.program_id(0)
    sources = moved_ref.shape[0] // groups
    total = sources * mics
    lane = lax.broadcasted_iota(jnp.int32, (1, LANES), 1)
    row8 = lax.broadcasted_iota(jnp.int32, (8, LANES), 0)
    spare = lane % halves == halves - 1
    of_block = lane // halves % blocks

    @pl.when(step == 0)
    def _():
        share = moved_ref.shape[0] // LANDINGS
        copies = []
        for i in range(LANDINGS):
            place = pl.ds(i * share, share)
            copies.append(pltpu.make_async_copy(moved_ref.at[place], land_ref.at[place], copied.at[i]))
            copies[-1].start()

        def carried(x):
            low = pltpu.roll(jnp.where(spare, x[0:8], 0.0), LANES - halves + 1, 1, stride=1, stride_axis=0)
            high = pltpu.roll(jnp.where(spare, x[8:16], 0.0), LANES - halves + 9, 1, stride=1, stride_axis=0)
            return jnp.sum(low + high, 0, keepdims=True)

        copies[0].wait()
        heads = [land_ref[group].astype(f32) for group in range(groups)]
        which = lax.broadcasted_iota(jnp.int32, (mics, LANES), 0)
        for group in range(groups):
            for b in range(blocks):
                mine = spare & (of_block == b) & (lane // (blocks * halves) == 0)
                number = jnp.where(which == halves, heads[group] * mics, jnp.where(which == halves + 1, heads[group], 0.0))
                start_ref[group * blocks + b] = jnp.sum(jnp.where(mine, number, 0.0)).astype(jnp.int32)
        for copy in copies[1:]:
            copy.wait()

        def one_source(i, after):
            source = sources - 1 - i
            before = []
            for group in range(groups):
                x = land_ref[source * groups + group].astype(f32)
                first = pl.multiple_of(source * mics, mics)
                wide_ref[group, pl.ds(first, mics - 8), :] = x[: mics - 8]
                wide_ref[group, pl.ds(first + mics - 8, 8), :] = x[mics - 8 :] + jnp.where(row8 == 7, after[group], 0.0)
                before.append(carried(x))
            return tuple(before)

        lax.fori_loop(0, sources, one_source, tuple(carried(x) for x in heads), unroll=8)
        for group in range(groups):
            wide_ref[group, total : total + PIECE, :] = wide_ref[group, 0:PIECE, :]
        sum_ref[...] = jnp.zeros(sum_ref.shape, f32)

    stacked = []
    for piece in range(BEAM_ROWS // PIECE):
        columns = []
        for group in range(groups):
            start = [(start_ref[group * blocks + b] + step * BEAM_ROWS + piece * PIECE) % total for b in range(blocks)]
            rows = [wide_ref[group, pl.ds(s, PIECE), :] for s in start]
            columns.append(jnp.where(of_block == 0, rows[0], rows[1]).astype(bf16))
        stacked.append(jnp.concatenate(columns, 1))
    sum_ref[...] += jnp.dot(steer_ref[...], jnp.concatenate(stacked, 0), preferred_element_type=f32)

    @pl.when(step == pl.num_programs(0) - 1)
    def _():
        points = out_ref.shape[1]
        slot = blocks * halves
        imaginary = lane // slot % 2 == 1
        for j in range(out_ref.shape[0]):
            power = jnp.zeros((points, LANES), f32)
            for group in range(groups):
                cols = slice(group * LANES, (group + 1) * LANES)
                by_cos = sum_ref[2 * j * points : (2 * j + 1) * points, cols]
                by_sin = sum_ref[(2 * j + 1) * points : (2 * j + 2) * points, cols]
                other = jnp.where(imaginary, -pltpu.roll(by_sin, slot, 1), pltpu.roll(by_sin, LANES - slot, 1))
                both = by_cos + other
                power = power + both * both
            power = jnp.where(~spare & (lane // (2 * slot) == j), power, 0.0)
            out_ref[j : j + 1, :] = jnp.sum(power.T, 0, keepdims=True) * scale


def beam(moved, steer, mics, blocks, halves, groups, points, scale):
    total = moved.shape[0] // groups * mics
    bins = steer.shape[0] // (2 * points)
    body = lambda *refs: beam_body(*refs, mics=mics, blocks=blocks, halves=halves, groups=groups, scale=scale)
    return pl.pallas_call(
        body,
        grid=(total // BEAM_ROWS,),
        out_shape=jax.ShapeDtypeStruct((bins, points), f32),
        in_specs=[
            pl.BlockSpec(memory_space=pl.ANY),
            pl.BlockSpec((steer.shape[0], BEAM_ROWS), lambda i: (0, i)),
        ],
        out_specs=pl.BlockSpec((bins, points), lambda i: (0, 0)),
        scratch_shapes=[
            pltpu.VMEM(moved.shape, bf16),
            pltpu.VMEM((groups, total + PIECE, LANES), f32),
            pltpu.SMEM((groups * blocks,), jnp.int32),
            pltpu.VMEM((steer.shape[0], groups * LANES), f32),
            pltpu.SemaphoreType.DMA((LANDINGS,)),
        ],
        name="beam",
    )(moved, steer)


def local(signal, offsets, fraction, radius, azimuth):
    blocks, mics, length = signal.shape
    sectors, groups = lax.axis_size("sector"), lax.axis_size("blk")
    owners = sectors * groups
    halves = length // HALF
    bins = HALF // owners
    spectra = local_spectra(signal, offsets, fraction, owners)
    moved = lax.all_to_all(spectra, ("sector", "blk"), split_axis=0, concat_axis=0, tiled=True)
    first = (lax.axis_index("sector") * groups + lax.axis_index("blk")) * bins
    total_mics = sectors * mics
    steer = steering(first, bins, radius, azimuth, total_mics)
    scale = 1.0 / (total_mics * blocks * (halves - 1) * groups)
    return beam(moved, steer, mics, blocks, halves, groups, radius.shape[0], scale)


def solution(mesh):
    return jax.shard_map(
        local,
        mesh=mesh,
        in_specs=(P("blk", "sector", None), P("blk"), P("blk", None), P(), P()),
        out_specs=P(("sector", "blk"), None),
        check_vma=False,
    )
```

```python
import math

import jax
import jax.numpy as jnp
import numpy as np
from jax import lax
from jax.experimental import pallas as pl
from jax.experimental.pallas import tpu as pltpu
from jax.sharding import PartitionSpec as P

NFFT = 1024
HALF = NFFT // 2
LANES = 128

wavenumber = 2.0
height = 0.5

f32 = jnp.float32
bf16 = jnp.bfloat16


def fourier_table(owners):
    sample = np.arange(NFFT)[:, None]
    per_owner = HALF // owners
    in_group = LANES // (2 * per_owner)
    column = np.arange(2 * HALF)[None, :]
    owner = column // LANES * in_group + column % in_group
    part = column // in_group % 2
    frequency = owner * per_owner + column % LANES // (2 * in_group)
    angle = (sample * frequency % NFFT) * (2.0 * math.pi / NFFT)
    window = 0.5 - 0.5 * np.cos(sample * (2.0 * math.pi / NFFT))
    value = np.where(part == 0, np.cos(angle), -np.sin(angle)) * window / math.sqrt(3.0 * NFFT / 8.0)
    return value.astype(np.float32).astype(bf16)


ROWS = 16
TABLE_COLS = 256


def gather_rows(signal_ref, fraction_ref, rows_ref):
    blocks, mics, length = signal_ref.shape
    halves = length // HALF
    row = lax.broadcasted_iota(jnp.int32, (mics, 1), 0)

    def place(part, b, segment):
        first = ((part * blocks + b) * halves + segment) * ROWS
        return slice(first, first + ROWS)

    for b in range(blocks):
        for h in range(halves):
            cols = slice(h * HALF, (h + 1) * HALF)
            weight = fraction_ref[b : b + 1, cols]
            here = signal_ref[b, :, cols].astype(f32)
            turned = pltpu.roll(here, mics - 1, 0)
            ending = jnp.where(row[:8] == 7, 0.0, turned[mics - 8 :])
            following = jnp.concatenate([turned[: mics - 8], ending], 0)
            mixed = ((1.0 - weight) * here + weight * following).astype(bf16)
            for part in range(mics // ROWS):
                piece = mixed[part * ROWS : (part + 1) * ROWS]
                if h < halves - 1:
                    rows_ref[place(part, b, h), :HALF] = piece
                if h > 0:
                    rows_ref[place(part, b, h - 1), HALF:] = piece
        share = jnp.zeros((ROWS, NFFT), f32)
        for segment in range(halves - 1):
            cols = slice(segment * HALF, segment * HALF + NFFT)
            first = fraction_ref[b : b + 1, cols] * signal_ref[b, 0:1, cols].astype(f32)
            share = jnp.where(row[:ROWS] == segment, first, share)
        rows_ref[place(0, b, halves - 1), :] = share.astype(bf16)
        for part in range(1, mics // ROWS):
            rows_ref[place(part, b, halves - 1), :] = jnp.zeros((ROWS, NFFT), bf16)


def spectra_body(offsets_ref, signal_ref, fraction_ref, table_ref, out_ref, rows_ref):
    blocks, mics, length = signal_ref.shape
    halves = length // HALF
    slot = blocks * halves
    lane = lax.broadcasted_iota(jnp.int32, (ROWS, LANES), 1)
    row = lax.broadcasted_iota(jnp.int32, (ROWS, LANES), 0)

    @pl.when(pl.program_id(0) == 0)
    def _():
        gather_rows(signal_ref, fraction_ref, rows_ref)

    for part in range(mics // ROWS):
        rows = rows_ref[part * slot * ROWS : (part + 1) * slot * ROWS, :]
        product = jnp.dot(rows, table_ref[...], preferred_element_type=f32)
        for tile in range(TABLE_COLS // LANES):
            pieces = [product[i * ROWS : (i + 1) * ROWS, tile * LANES : (tile + 1) * LANES] for i in range(slot)]
            if part == 1:
                for b in range(blocks):
                    i = b * halves + halves - 1
                    hop = (offsets_ref[b] // mics).astype(f32)
                    within = (offsets_ref[b] % mics).astype(f32)
                    pieces[i] = jnp.where(row == 0, hop, jnp.where(row == 1, within, pieces[i]))
            pieces = [piece.astype(bf16) for piece in pieces]
            pieces = [pltpu.roll(pieces[i], i, 1) if i else pieces[i] for i in range(slot)]
            pieces = [pieces[-i % slot] for i in range(slot)]
            step = 1
            while step < slot:
                odd = lane // step % 2 == 1
                pieces = [jnp.where(odd, pieces[(i - step) % slot], pieces[i]) for i in range(slot)]
                step *= 2
            pieces = [pltpu.roll(pieces[i], LANES - i, 1) if i else pieces[i] for i in range(slot)]
            for i in range(slot):
                out_ref[tile * slot + i, part * ROWS : (part + 1) * ROWS, :] = pieces[i].astype(bf16)


def local_spectra(signal, offsets, fraction, owners):
    blocks, mics, length = signal.shape
    rows = mics * blocks * (length // HALF)
    per_step = owners * TABLE_COLS // NFFT
    return pl.pallas_call(
        spectra_body,
        grid=(NFFT // TABLE_COLS,),
        out_shape=jax.ShapeDtypeStruct((owners, mics, LANES), bf16),
        in_specs=[
            pl.BlockSpec(memory_space=pltpu.SMEM),
            pl.BlockSpec(signal.shape, lambda i: (0, 0, 0)),
            pl.BlockSpec(fraction.shape, lambda i: (0, 0)),
            pl.BlockSpec((NFFT, TABLE_COLS), lambda i: (0, i)),
        ],
        out_specs=pl.BlockSpec((per_step, mics, LANES), lambda i: (i, 0, 0)),
        scratch_shapes=[pltpu.VMEM((rows, NFFT), bf16)],
        name="spectra",
    )(offsets, signal, fraction, jnp.asarray(fourier_table(owners)))


def cos_sin(phase):
    turns = jnp.round(phase * (1.0 / math.pi))
    rest = phase - turns * 3.140625
    rest = rest - turns * 9.67502593994140625e-4
    rest = rest - turns * 1.509957990978376432e-7
    half = turns * 0.5
    sign = 1.0 - 4.0 * (half - jnp.floor(half))
    square = rest * rest
    cosine = 1.0 / math.factorial(12)
    for order in (10, 8, 6, 4, 2, 0):
        cosine = cosine * square + (-1.0) ** (order // 2) / math.factorial(order)
    sine = -1.0 / math.factorial(11)
    for order in (9, 7, 5, 3, 1):
        sine = sine * square + (-1.0) ** (order // 2) / math.factorial(order)
    return sign * cosine, sign * rest * sine


STEER_COLS = 512


def steer_body(first_ref, cycle_ref, base_ref, across_ref, along_ref, out_ref):
    points = base_ref.shape[0]
    bins = out_ref.shape[0] // (2 * points)
    first = first_ref[0]
    cycle_cos = cycle_ref[0:1, :]
    cycle_sin = cycle_ref[1:2, :]

    def rows16(i, _):
        rows = pl.ds(pl.multiple_of(i * 16, 16), 16)
        squared = base_ref[rows, :] - 2.0 * (cycle_cos * across_ref[rows, :] + cycle_sin * along_ref[rows, :])
        distance = jnp.sqrt(squared)
        for j in range(bins):
            phase = wavenumber * (first + j).astype(f32) * distance
            cosine, sine = cos_sin(phase)
            place = pl.multiple_of(2 * j * points + i * 16, 16)
            out_ref[pl.ds(place, 16), :] = cosine.astype(bf16)
            place = pl.multiple_of((2 * j + 1) * points + i * 16, 16)
            out_ref[pl.ds(place, 16), :] = sine.astype(bf16)
        return 0

    lax.fori_loop(0, points // 16, rows16, 0)


def steering(first, bins, radius, azimuth, total_mics):
    turn = lax.iota(jnp.int32, total_mics).astype(f32) * (2.0 * math.pi / total_mics)
    cycle = jnp.stack([jnp.cos(turn), jnp.sin(turn)])
    points = radius.shape[0]
    base = (1.0 + height * height + radius * radius)[:, None]
    across = (radius * jnp.cos(azimuth))[:, None]
    along = (radius * jnp.sin(azimuth))[:, None]
    column = pl.BlockSpec((points, 1), lambda i: (0, 0))
    return pl.pallas_call(
        steer_body,
        grid=(total_mics // STEER_COLS,),
        out_shape=jax.ShapeDtypeStruct((bins * 2 * points, total_mics), bf16),
        in_specs=[
            pl.BlockSpec(memory_space=pltpu.SMEM),
            pl.BlockSpec((2, STEER_COLS), lambda i: (0, i)),
            column,
            column,
            column,
        ],
        out_specs=pl.BlockSpec((bins * 2 * points, STEER_COLS), lambda i: (0, i)),
        name="steer",
    )(first.reshape(1), cycle, base, across, along)


BEAM_ROWS = 1024
PIECE = 512


def beam_body(moved_ref, steer_ref, out_ref, wide_ref, start_ref, sum_ref, *, mics, blocks, halves, groups, scale):
    step = pl.program_id(0)
    sources = moved_ref.shape[0] // groups
    total = sources * mics
    lane = lax.broadcasted_iota(jnp.int32, (1, LANES), 1)
    row8 = lax.broadcasted_iota(jnp.int32, (8, LANES), 0)
    spare = lane % halves == halves - 1
    of_block = lane // halves % blocks

    @pl.when(step == 0)
    def _():
        def carried(x):
            low = pltpu.roll(jnp.where(spare, x[0:8], 0.0), LANES - halves + 1, 1, stride=1, stride_axis=0)
            high = pltpu.roll(jnp.where(spare, x[8:16], 0.0), LANES - halves + 9, 1, stride=1, stride_axis=0)
            return jnp.sum(low + high, 0, keepdims=True)

        heads = [moved_ref[group].astype(f32) for group in range(groups)]
        which = lax.broadcasted_iota(jnp.int32, (mics, LANES), 0)
        for group in range(groups):
            for b in range(blocks):
                mine = spare & (of_block == b) & (lane // (blocks * halves) == 0)
                number = jnp.where(which == halves, heads[group] * mics, jnp.where(which == halves + 1, heads[group], 0.0))
                start_ref[group * blocks + b] = jnp.sum(jnp.where(mine, number, 0.0)).astype(jnp.int32)

        def one_source(i, after):
            source = sources - 1 - i
            before = []
            for group in range(groups):
                x = moved_ref[source * groups + group].astype(f32)
                first = pl.multiple_of(source * mics, mics)
                wide_ref[group, pl.ds(first, mics - 8), :] = x[: mics - 8]
                wide_ref[group, pl.ds(first + mics - 8, 8), :] = x[mics - 8 :] + jnp.where(row8 == 7, after[group], 0.0)
                before.append(carried(x))
            return tuple(before)

        lax.fori_loop(0, sources, one_source, tuple(carried(x) for x in heads), unroll=32)
        for group in range(groups):
            wide_ref[group, total : total + PIECE, :] = wide_ref[group, 0:PIECE, :]
        sum_ref[...] = jnp.zeros(sum_ref.shape, f32)

    stacked = []
    for piece in range(BEAM_ROWS // PIECE):
        columns = []
        for group in range(groups):
            start = [(start_ref[group * blocks + b] + step * BEAM_ROWS + piece * PIECE) % total for b in range(blocks)]
            rows = [wide_ref[group, pl.ds(s, PIECE), :] for s in start]
            columns.append(jnp.where(of_block == 0, rows[0], rows[1]).astype(bf16))
        stacked.append(jnp.concatenate(columns, 1))
    sum_ref[...] += jnp.dot(steer_ref[...], jnp.concatenate(stacked, 0), preferred_element_type=f32)

    @pl.when(step == pl.num_programs(0) - 1)
    def _():
        points = out_ref.shape[1]
        slot = blocks * halves
        imaginary = lane // slot % 2 == 1
        for j in range(out_ref.shape[0]):
            power = jnp.zeros((points, LANES), f32)
            for group in range(groups):
                cols = slice(group * LANES, (group + 1) * LANES)
                by_cos = sum_ref[2 * j * points : (2 * j + 1) * points, cols]
                by_sin = sum_ref[(2 * j + 1) * points : (2 * j + 2) * points, cols]
                other = jnp.where(imaginary, -pltpu.roll(by_sin, slot, 1), pltpu.roll(by_sin, LANES - slot, 1))
                both = by_cos + other
                power = power + both * both
            power = jnp.where(~spare & (lane // (2 * slot) == j), power, 0.0)
            out_ref[j : j + 1, :] = jnp.sum(power.T, 0, keepdims=True) * scale


def beam(moved, steer, mics, blocks, halves, groups, points, scale):
    total = moved.shape[0] // groups * mics
    bins = steer.shape[0] // (2 * points)
    body = lambda *refs: beam_body(*refs, mics=mics, blocks=blocks, halves=halves, groups=groups, scale=scale)
    return pl.pallas_call(
        body,
        grid=(total // BEAM_ROWS,),
        out_shape=jax.ShapeDtypeStruct((bins, points), f32),
        in_specs=[
            pl.BlockSpec(memory_space=pltpu.VMEM),
            pl.BlockSpec((steer.shape[0], BEAM_ROWS), lambda i: (0, i)),
        ],
        out_specs=pl.BlockSpec((bins, points), lambda i: (0, 0)),
        scratch_shapes=[
            pltpu.VMEM((groups, total + PIECE, LANES), f32),
            pltpu.SMEM((groups * blocks,), jnp.int32),
            pltpu.VMEM((steer.shape[0], groups * LANES), f32),
        ],
        name="beam",
    )(moved, steer)


def local(signal, offsets, fraction, radius, azimuth):
    blocks, mics, length = signal.shape
    sectors, groups = lax.axis_size("sector"), lax.axis_size("blk")
    owners = sectors * groups
    halves = length // HALF
    bins = HALF // owners
    spectra = local_spectra(signal, offsets, fraction, owners)
    moved = lax.all_to_all(spectra, ("sector", "blk"), split_axis=0, concat_axis=0, tiled=True)
    moved = pltpu.with_memory_space_constraint(moved, pltpu.VMEM)
    first = (lax.axis_index("sector") * groups + lax.axis_index("blk")) * bins
    total_mics = sectors * mics
    steer = steering(first, bins, radius, azimuth, total_mics)
    scale = 1.0 / (total_mics * blocks * (halves - 1) * groups)
    return beam(moved, steer, mics, blocks, halves, groups, radius.shape[0], scale)


def solution(mesh):
    return jax.shard_map(
        local,
        mesh=mesh,
        in_specs=(P("blk", "sector", None), P("blk"), P("blk", None), P(), P()),
        out_specs=P(("sector", "blk"), None),
        check_vma=False,
    )
```

```python
import math

import jax
import jax.numpy as jnp
import numpy as np
from jax import lax
from jax.experimental import pallas as pl
from jax.experimental.pallas import tpu as pltpu
from jax.sharding import PartitionSpec as P

NFFT = 1024
HALF = NFFT // 2
LANES = 128

wavenumber = 2.0
height = 0.5

f32 = jnp.float32
bf16 = jnp.bfloat16


def fourier_table(owners):
    sample = np.arange(NFFT)[:, None]
    per_owner = HALF // owners
    in_group = LANES // (2 * per_owner)
    column = np.arange(2 * HALF)[None, :]
    owner = column // LANES * in_group + column % in_group
    part = column // in_group % 2
    frequency = owner * per_owner + column % LANES // (2 * in_group)
    angle = (sample * frequency % NFFT) * (2.0 * math.pi / NFFT)
    window = 0.5 - 0.5 * np.cos(sample * (2.0 * math.pi / NFFT))
    value = np.where(part == 0, np.cos(angle), -np.sin(angle)) * window / math.sqrt(3.0 * NFFT / 8.0)
    return value.astype(np.float32).astype(bf16)


ROWS = 16
TABLE_COLS = 256


def gather_rows(b, signal_ref, fraction_ref, rows_ref):
    blocks, mics, length = signal_ref.shape
    halves = length // HALF
    row = lax.broadcasted_iota(jnp.int32, (mics, 1), 0)

    def place(part, b, segment):
        first = ((part * blocks + b) * halves + segment) * ROWS
        return slice(first, first + ROWS)

    for h in range(halves):
        cols = slice(h * HALF, (h + 1) * HALF)
        weight = fraction_ref[b : b + 1, cols]
        here = signal_ref[b, :, cols].astype(f32)
        turned = pltpu.roll(here, mics - 1, 0)
        ending = jnp.where(row[:8] == 7, 0.0, turned[mics - 8 :])
        following = jnp.concatenate([turned[: mics - 8], ending], 0)
        mixed = ((1.0 - weight) * here + weight * following).astype(bf16)
        for part in range(mics // ROWS):
            piece = mixed[part * ROWS : (part + 1) * ROWS]
            if h < halves - 1:
                rows_ref[place(part, b, h), :HALF] = piece
            if h > 0:
                rows_ref[place(part, b, h - 1), HALF:] = piece
    share = jnp.zeros((ROWS, NFFT), f32)
    for segment in range(halves - 1):
        cols = slice(segment * HALF, segment * HALF + NFFT)
        first = fraction_ref[b : b + 1, cols] * signal_ref[b, 0:1, cols].astype(f32)
        share = jnp.where(row[:ROWS] == segment, first, share)
    rows_ref[place(0, b, halves - 1), :] = share.astype(bf16)
    for part in range(1, mics // ROWS):
        rows_ref[place(part, b, halves - 1), :] = jnp.zeros((ROWS, NFFT), bf16)


def spectra_body(offsets_ref, signal_hbm, fraction_hbm, table_hbm, out_hbm, signal_ref, fraction_ref, table_ref, rows_ref, out_ref, copied):
    blocks, mics, length = signal_ref.shape
    halves = length // HALF
    slot = blocks * halves
    lane = lax.broadcasted_iota(jnp.int32, (ROWS, LANES), 1)
    row = lax.broadcasted_iota(jnp.int32, (ROWS, LANES), 0)

    pairs = [(fraction_hbm, fraction_ref)]
    pairs += [(signal_hbm.at[b], signal_ref.at[b]) for b in range(blocks)]
    pairs += [(table_hbm.at[i], table_ref.at[i]) for i in range(table_ref.shape[0])]
    copies = [pltpu.make_async_copy(source, target, copied.at[i]) for i, (source, target) in enumerate(pairs)]
    for copy in copies:
        copy.start()
    copies[0].wait()
    for b in range(blocks):
        copies[1 + b].wait()
        gather_rows(b, signal_ref, fraction_ref, rows_ref)
    columns = table_ref.shape[0]
    share = out_ref.shape[0] // columns
    leaving = []
    for i in range(columns):
        copies[1 + blocks + i].wait()
        spectra_columns(i, offsets_ref, table_ref, rows_ref, out_ref, lane, row, blocks, mics, halves, slot)
        place = pl.ds(i * share, share)
        leaving.append(pltpu.make_async_copy(out_ref.at[place], out_hbm.at[place], copied.at[len(copies) + i]))
        leaving[-1].start()
    for copy in leaving:
        copy.wait()


def spectra_columns(column, offsets_ref, table_ref, rows_ref, out_ref, lane, row, blocks, mics, halves, slot):
    first = column * (TABLE_COLS // LANES) * slot
    for part in range(mics // ROWS):
        rows = rows_ref[part * slot * ROWS : (part + 1) * slot * ROWS, :]
        product = jnp.dot(rows, table_ref[column], preferred_element_type=f32)
        for tile in range(TABLE_COLS // LANES):
            pieces = [product[i * ROWS : (i + 1) * ROWS, tile * LANES : (tile + 1) * LANES] for i in range(slot)]
            if part == 1:
                for b in range(blocks):
                    i = b * halves + halves - 1
                    hop = (offsets_ref[b] // mics).astype(f32)
                    within = (offsets_ref[b] % mics).astype(f32)
                    pieces[i] = jnp.where(row == 0, hop, jnp.where(row == 1, within, pieces[i]))
            pieces = [piece.astype(bf16) for piece in pieces]
            pieces = [pltpu.roll(pieces[i], i, 1) if i else pieces[i] for i in range(slot)]
            pieces = [pieces[-i % slot] for i in range(slot)]
            step = 1
            while step < slot:
                odd = lane // step % 2 == 1
                pieces = [jnp.where(odd, pieces[(i - step) % slot], pieces[i]) for i in range(slot)]
                step *= 2
            pieces = [pltpu.roll(pieces[i], LANES - i, 1) if i else pieces[i] for i in range(slot)]
            for i in range(slot):
                out_ref[first + tile * slot + i, part * ROWS : (part + 1) * ROWS, :] = pieces[i].astype(bf16)


def local_spectra(signal, offsets, fraction, owners):
    blocks, mics, length = signal.shape
    rows = mics * blocks * (length // HALF)
    table = fourier_table(owners).reshape(NFFT, NFFT // TABLE_COLS, TABLE_COLS).transpose(1, 0, 2)
    hbm = pl.BlockSpec(memory_space=pltpu.HBM)
    return pl.pallas_call(
        spectra_body,
        out_shape=jax.ShapeDtypeStruct((owners, mics, LANES), bf16),
        in_specs=[pl.BlockSpec(memory_space=pltpu.SMEM), hbm, hbm, hbm],
        out_specs=hbm,
        scratch_shapes=[
            pltpu.VMEM(signal.shape, bf16),
            pltpu.VMEM(fraction.shape, f32),
            pltpu.VMEM(table.shape, bf16),
            pltpu.VMEM((rows, NFFT), bf16),
            pltpu.VMEM((owners, mics, LANES), bf16),
            pltpu.SemaphoreType.DMA((1 + blocks + 2 * table.shape[0],)),
        ],
        name="spectra",
    )(offsets, signal, fraction, jnp.asarray(table))


def cos_sin(phase):
    turns = jnp.round(phase * (1.0 / math.pi))
    rest = phase - turns * 3.140625
    rest = rest - turns * 9.67502593994140625e-4
    rest = rest - turns * 1.509957990978376432e-7
    half = turns * 0.5
    sign = 1.0 - 4.0 * (half - jnp.floor(half))
    square = rest * rest
    cosine = 1.0 / math.factorial(12)
    for order in (10, 8, 6, 4, 2, 0):
        cosine = cosine * square + (-1.0) ** (order // 2) / math.factorial(order)
    sine = -1.0 / math.factorial(11)
    for order in (9, 7, 5, 3, 1):
        sine = sine * square + (-1.0) ** (order // 2) / math.factorial(order)
    return sign * cosine, sign * rest * sine


STEER_COLS = 1024


def steer_body(first_ref, cycle_ref, base_ref, across_ref, along_ref, out_ref):
    points = base_ref.shape[0]
    bins = out_ref.shape[1] // (2 * points)
    first = first_ref[0]
    cycle_cos = cycle_ref[0:1, :]
    cycle_sin = cycle_ref[1:2, :]

    def rows16(i, _):
        rows = pl.ds(pl.multiple_of(i * 16, 16), 16)
        squared = base_ref[rows, :] - 2.0 * (cycle_cos * across_ref[rows, :] + cycle_sin * along_ref[rows, :])
        distance = jnp.sqrt(squared)
        for j in range(bins):
            phase = wavenumber * (first + j).astype(f32) * distance
            cosine, sine = cos_sin(phase)
            place = pl.multiple_of(2 * j * points + i * 16, 16)
            out_ref[0, pl.ds(place, 16), :] = cosine.astype(bf16)
            place = pl.multiple_of((2 * j + 1) * points + i * 16, 16)
            out_ref[0, pl.ds(place, 16), :] = sine.astype(bf16)
        return 0

    lax.fori_loop(0, points // 16, rows16, 0)


def steering(first, bins, radius, azimuth, total_mics):
    turn = lax.iota(jnp.int32, total_mics).astype(f32) * (2.0 * math.pi / total_mics)
    cycle = jnp.stack([jnp.cos(turn), jnp.sin(turn)])
    points = radius.shape[0]
    base = (1.0 + height * height + radius * radius)[:, None]
    across = (radius * jnp.cos(azimuth))[:, None]
    along = (radius * jnp.sin(azimuth))[:, None]
    column = pl.BlockSpec((points, 1), lambda i: (0, 0))
    return pl.pallas_call(
        steer_body,
        grid=(total_mics // STEER_COLS,),
        out_shape=jax.ShapeDtypeStruct((total_mics // STEER_COLS, bins * 2 * points, STEER_COLS), bf16),
        in_specs=[
            pl.BlockSpec(memory_space=pltpu.SMEM),
            pl.BlockSpec((2, STEER_COLS), lambda i: (0, i)),
            column,
            column,
            column,
        ],
        out_specs=pl.BlockSpec((1, bins * 2 * points, STEER_COLS), lambda i: (i, 0, 0)),
        name="steer",
    )(first.reshape(1), cycle, base, across, along)


PIECE = 512


def beam_body(moved_ref, steer_hbm, out_ref, wide_ref, rows_ref, sum_ref, steer_ref, copied, *, mics, blocks, halves, groups, scale):
    chunks = steer_ref.shape[0]
    copies = [pltpu.make_async_copy(steer_hbm.at[i], steer_ref.at[i], copied.at[i]) for i in range(chunks)]
    for copy in copies:
        copy.start()
    sources = moved_ref.shape[0] // groups
    total = sources * mics
    lane = lax.broadcasted_iota(jnp.int32, (1, LANES), 1)
    row8 = lax.broadcasted_iota(jnp.int32, (8, LANES), 0)
    spare = lane % halves == halves - 1
    of_block = lane // halves % blocks

    def carried(x):
        low = pltpu.roll(jnp.where(spare, x[0:8], 0.0), LANES - halves + 1, 1, stride=1, stride_axis=0)
        high = pltpu.roll(jnp.where(spare, x[8:16], 0.0), LANES - halves + 9, 1, stride=1, stride_axis=0)
        return jnp.sum(low + high, 0, keepdims=True)

    heads = [moved_ref[group].astype(f32) for group in range(groups)]
    starts = {}
    which = lax.broadcasted_iota(jnp.int32, (mics, LANES), 0)
    for group in range(groups):
        for b in range(blocks):
            mine = spare & (of_block == b) & (lane // (blocks * halves) == 0)
            number = jnp.where(which == halves, heads[group] * mics, jnp.where(which == halves + 1, heads[group], 0.0))
            starts[group, b] = jnp.sum(jnp.where(mine, number, 0.0)).astype(jnp.int32)

    def one_source(i, after):
        source = sources - 1 - i
        before = []
        for group in range(groups):
            x = moved_ref[source * groups + group].astype(f32)
            first = pl.multiple_of(source * mics, mics)
            wide_ref[group, pl.ds(first, mics - 8), :] = x[: mics - 8]
            wide_ref[group, pl.ds(first + mics - 8, 8), :] = x[mics - 8 :] + jnp.where(row8 == 7, after[group], 0.0)
            before.append(carried(x))
        return tuple(before)

    lax.fori_loop(0, sources, one_source, tuple(carried(x) for x in heads), unroll=32)
    for group in range(groups):
        wide_ref[group, total : total + PIECE, :] = wide_ref[group, 0:PIECE, :]

    depth = total // chunks
    for piece in range(total // PIECE):
        for group in range(groups):
            begin = [(starts[group, b] + piece * PIECE) % total for b in range(blocks)]
            rows = [wide_ref[group, pl.ds(s, PIECE), :] for s in begin]
            mixed = jnp.where(of_block == 0, rows[0], rows[1]).astype(bf16)
            rows_ref[piece * PIECE : (piece + 1) * PIECE, group * LANES : (group + 1) * LANES] = mixed
        end = (piece + 1) * PIECE
        if end % depth == 0:
            chunk = end // depth - 1
            copies[chunk].wait()
            product = jnp.dot(steer_ref[chunk], rows_ref[end - depth : end, :], preferred_element_type=f32)
            if chunk == 0:
                sum_ref[...] = product
            else:
                sum_ref[...] += product

    points = out_ref.shape[1]
    slot = blocks * halves
    imaginary = lane // slot % 2 == 1
    for j in range(out_ref.shape[0]):
        power = jnp.zeros((points, LANES), f32)
        for group in range(groups):
            cols = slice(group * LANES, (group + 1) * LANES)
            by_cos = sum_ref[2 * j * points : (2 * j + 1) * points, cols]
            by_sin = sum_ref[(2 * j + 1) * points : (2 * j + 2) * points, cols]
            other = jnp.where(imaginary, -pltpu.roll(by_sin, slot, 1), pltpu.roll(by_sin, LANES - slot, 1))
            both = by_cos + other
            power = power + both * both
        power = jnp.where(~spare & (lane // (2 * slot) == j), power, 0.0)
        out_ref[j : j + 1, :] = jnp.sum(power.T, 0, keepdims=True) * scale


def beam(moved, steer, mics, blocks, halves, groups, points, scale):
    total = moved.shape[0] // groups * mics
    chunks, rows, depth = steer.shape
    bins = rows // (2 * points)
    body = lambda *refs: beam_body(*refs, mics=mics, blocks=blocks, halves=halves, groups=groups, scale=scale)
    vmem = pl.BlockSpec(memory_space=pltpu.VMEM)
    return pl.pallas_call(
        body,
        out_shape=jax.ShapeDtypeStruct((bins, points), f32),
        in_specs=[vmem, pl.BlockSpec(memory_space=pltpu.HBM)],
        out_specs=vmem,
        scratch_shapes=[
            pltpu.VMEM((groups, total + PIECE, LANES), f32),
            pltpu.VMEM((total, groups * LANES), bf16),
            pltpu.VMEM((rows, groups * LANES), f32),
            pltpu.VMEM(steer.shape, bf16),
            pltpu.SemaphoreType.DMA((chunks,)),
        ],
        name="beam",
    )(moved, steer)


def local(signal, offsets, fraction, radius, azimuth):
    blocks, mics, length = signal.shape
    sectors, groups = lax.axis_size("sector"), lax.axis_size("blk")
    owners = sectors * groups
    halves = length // HALF
    bins = HALF // owners
    spectra = local_spectra(signal, offsets, fraction, owners)
    moved = lax.all_to_all(spectra, ("sector", "blk"), split_axis=0, concat_axis=0, tiled=True)
    moved = pltpu.with_memory_space_constraint(moved, pltpu.VMEM)
    first = (lax.axis_index("sector") * groups + lax.axis_index("blk")) * bins
    total_mics = sectors * mics
    steer = steering(first, bins, radius, azimuth, total_mics)
    scale = 1.0 / (total_mics * blocks * (halves - 1) * groups)
    return beam(moved, steer, mics, blocks, halves, groups, radius.shape[0], scale)


def solution(mesh):
    return jax.shard_map(
        local,
        mesh=mesh,
        in_specs=(P("blk", "sector", None), P("blk"), P("blk", None), P(), P()),
        out_specs=P(("sector", "blk"), None),
        check_vma=False,
    )
```
